128 devices in a mesh: row: 8 (over z, y_lo), pair: 16 (over x, y_hi, core).
Axes of the slice: x: 4, y: 4 (y_hi: 2, y_lo: 2; y = y_hi * 2 + y_lo), z: 4, core: 2. Of those that a mesh axis runs over, the one named last changes fastest.
Arguments:
- snapshots: float32 [32768, 2048], P(('row', 'pair')), may hold values from -640 to 640
- start_order: int32 [32], replicated, may hold values from 0 to 31, each once
Outputs:
- rotated: float32 [32768, 2048], P('row', 'pair')
The draws below stay inside these ranges and needn't reach their ends.
Inputs may be any that keep to these rules, and one draw needn't show every extreme that they name: `start_order`: each of the 32 block numbers appears once.
All inputs are finite; a program needn't handle non-finite values.
Results may differ from the reference program's by a relative error of at most 0.0003.
Values sent between devices are 32-bit elements; how exact they have to be, the bound alone decides.
A program may use at most 64 MiB of HBM per device.

```python
import math
import jax
import jax.numpy as jnp
from jax import lax

ROWS_DEV = 4096
STEPS = 12
ROOT_STEPS = 3
BLOCKS = 32
COLUMNS = 2048
ROWS = 32768
N_ROW = 8


def draw_snapshots(key, part):
    keys = jax.random.split(jax.random.fold_in(key, 17), 5)
    row_ids = jnp.arange(ROWS)
    region = row_ids // ROWS_DEV
    modes = jax.random.truncated_normal(keys[0], -3.0, 3.0, (ROWS, 2), jnp.float32)
    loads = jax.random.truncated_normal(keys[1], -3.0, 3.0, (N_ROW, 2, COLUMNS), jnp.float32)
    noise = jax.random.truncated_normal(keys[2], -3.0, 3.0, (ROWS, COLUMNS), jnp.float32)
    growth = 3.0
    load_first = loads[:, 0, :][region]
    load_second = loads[:, 1, :][region]
    rough = jax.random.uniform(keys[3], (ROWS, 1), jnp.float32, 0.7, 1.3)
    row_scale = jnp.exp(math.log(growth) * row_ids.astype(jnp.float32) / ROWS)[:, None] * rough
    column_scale = jnp.exp(jax.random.uniform(keys[4], (1, COLUMNS), jnp.float32, math.log(0.3), math.log(3.0)))
    values = modes[:, 0:1] * load_first + modes[:, 1:2] * load_second + noise
    return (row_scale * column_scale * values).astype(jnp.float32)


def setup_inputs(seed: int = 0) -> dict:
    key_of = jax.random.split(jax.random.key(seed), 3)
    return {
        "snapshots": draw_snapshots(jax.random.fold_in(key_of[2], 71), 0),
        "start_order": jax.random.permutation(key_of[1], BLOCKS).astype(jnp.int32),
    }


def matmul_high(left, right):
    return jnp.matmul(left, right, precision=lax.Precision.HIGHEST)

def rotation(norms, cross):
    half_width = cross.shape[-1]
    inverse_norm = lax.rsqrt(norms + 1e-06)
    cross_block = cross * inverse_norm[..., :half_width, None] * inverse_norm[..., None, half_width:]
    frobenius = jnp.sqrt(lax.optimization_barrier(jnp.sum(cross_block * cross_block, axis=(-2, -1), keepdims=True)))
    coupling = cross_block / (1.0 + frobenius)
    zero_block = jnp.zeros_like(coupling)
    upper = jnp.concatenate([zero_block, coupling], axis=-1)
    lower = jnp.concatenate([-jnp.swapaxes(coupling, -1, -2), zero_block], axis=-1)
    skew_matrix = jnp.concatenate([upper, lower], axis=-2)
    full_shape = skew_matrix.shape
    identity = jnp.broadcast_to(jnp.eye(2 * half_width, dtype=cross.dtype), full_shape)
    current = (identity - matmul_high(skew_matrix, skew_matrix)) * 0.5
    inverse_root = identity
    for root_number in range(ROOT_STEPS):
        correction = 1.5 * identity - 0.5 * matmul_high(inverse_root, current)
        current = matmul_high(current, correction)
        inverse_root = matmul_high(correction, inverse_root)
    return matmul_high(identity + skew_matrix, inverse_root) * (1.0 / math.sqrt(2.0))

def reference(snapshots, start_order):
    total_rows = snapshots.shape[0]
    block_count = start_order.shape[0]
    block_width = snapshots.shape[1] // block_count
    slot_count = block_count // 2
    arranged = jnp.take(snapshots.reshape(total_rows, block_count, block_width), start_order.astype(jnp.int32), axis=1)
    slab_state = arranged.reshape(total_rows, slot_count, 2 * block_width)

    def tournament_step(step_number, slab_state):
        cross = jnp.einsum('rpi,rpj->pij', slab_state[:, :, :block_width], slab_state[:, :, block_width:], precision=lax.Precision.HIGHEST)
        norms = lax.optimization_barrier(jnp.sum(slab_state * slab_state, axis=0))
        rotated = jnp.einsum('rpi,pij->rpj', slab_state, rotation(norms, cross), precision=lax.Precision.HIGHEST)
        first_block = rotated[:, :, :block_width]
        second = rotated[:, :, block_width:]
        new_first = jnp.concatenate([first_block[:, :1], second[:, :1], first_block[:, 1:slot_count - 1]], axis=1)
        new_second = jnp.concatenate([second[:, 1:], first_block[:, slot_count - 1:]], axis=1)
        return jnp.concatenate([new_first, new_second], axis=2)
    final_state = lax.fori_loop(0, STEPS, tournament_step, slab_state)
    return final_state.reshape(total_rows, slot_count * 2 * block_width)
```

```python
import math

import jax
import jax.numpy as jnp
from jax import lax
from jax.experimental import pallas as pl
from jax.experimental.pallas import tpu as pltpu
from jax.sharding import PartitionSpec as P

STEPS = 12
CHIPS = 8
SLOTS = 8
WIDTH = 64
PART = 40
MESH = pl.DeviceIdType.MESH
BF = jnp.bfloat16
F32 = jnp.float32
NT = (((1,), (1,)), ((), ()))


def split(x):
    high = x.astype(BF)
    return high, (x - high.astype(F32)).astype(BF)


def product(left, right):
    wide = jnp.concatenate(right, axis=1)
    y = jnp.dot(
        jnp.concatenate(left, axis=1), jnp.concatenate([wide, wide], axis=0), preferred_element_type=F32
    )
    return y[:, 0:128] + y[:, 128:256]


def tree(pieces):
    while len(pieces) > 1:
        pieces = [a + b for a, b in zip(pieces[::2], pieces[1::2])]
    return pieces[0]


def kernel(
    order_ref, xt_ref, out_ref,
    first0, first1, second0, second1, export, arrive, outbox, inbox, part, gather1, gather2, total, turn, final,
    send1, recv1, send2, recv2, send3, recv3, sendx, recvx, sendb, recvb, sendf, recvf,
):
    row = lax.axis_index("row")
    pair = lax.axis_index("pair")
    z, y_low = row // 2, row % 2
    chip, core = pair // 2, pair % 2
    x, y_high = chip // 2, chip % 2
    side = (y_low + y_high) % 2
    sibling = pair + 1 - 2 * core
    firsts, seconds = (first0, first1), (second0, second1)
    me1 = x * 2 + side
    me2 = z * 2 + y_high

    def sharer(j):
        return (z * 2 + (j + y_high) % 2, ((j // 2) * 2 + y_high) * 2 + core)

    def holder(j):
        return ((j // 2) * 2 + (side + j) % 2, (x * 2 + j % 2) * 2 + core)

    lanes = xt_ref.shape[2]
    here = pl.ds(pl.multiple_of(core * lanes, lanes), lanes)
    there = pl.ds(pl.multiple_of((1 - core) * lanes, lanes), lanes)

    barrier = pltpu.get_barrier_semaphore()

    def greet(device):
        pl.semaphore_signal(barrier, inc=1, device_id=device, device_id_type=MESH)

    for d in range(1, 8):
        greet(sharer((me1 + d) % 8))
        greet(holder((me2 + d) % 8))
    for d in range(1, 2 * CHIPS):
        greet((row, (pair + d) % (2 * CHIPS)))

    def position(owner, block):
        plain = 2 * (block % SLOTS) + block // SLOTS
        return plain + owner * (31 - 2 * plain)

    for b in range(2 * SLOTS):
        outbox[b] = xt_ref[order_ref[position(1 - core, b)]]
    pl.semaphore_wait(barrier, 14 + 2 * CHIPS - 1)
    swap = pltpu.make_async_remote_copy(
        src_ref=outbox, dst_ref=inbox, send_sem=sendb, recv_sem=recvb,
        device_id=(row, sibling), device_id_type=MESH,
    )
    swap.start()
    for b in range(2 * SLOTS):
        high, low = split(xt_ref[order_ref[position(core, b)]])
        state = first0 if b < SLOTS else second0
        state[b % SLOTS, 0:WIDTH, here] = high
        state[b % SLOTS, WIDTH:, here] = low
    swap.wait()
    for b in range(2 * SLOTS):
        high, low = split(inbox[b])
        state = first0 if b < SLOTS else second0
        state[b % SLOTS, 0:WIDTH, there] = high
        state[b % SLOTS, WIDTH:, there] = low

    lane32 = lax.broadcasted_iota(jnp.int32, (32, 128), 1)
    lane64 = lax.broadcasted_iota(jnp.int32, (64, 128), 1)
    sub64 = lax.broadcasted_iota(jnp.int32, (64, 128), 0)
    unit = (
        lax.broadcasted_iota(jnp.int32, (128, 128), 0)
        == lax.broadcasted_iota(jnp.int32, (128, 128), 1)
    ).astype(F32)
    ones = jnp.ones((8, 256), BF)
    minus_sign = (2 * core - 1).astype(F32)

    def bulk(buffer, sem):
        return pltpu.make_async_copy(buffer, buffer, sem)

    def crossing(now, j):
        a = firsts[now][j]
        b = seconds[now][j]
        grown = lax.dot_general(a, b, NT, preferred_element_type=F32)
        grown = grown[0:64] + grown[64:128]
        both = grown + pltpu.roll(grown, 64, 1)
        part[now, j, 0:32] = jnp.where(lane32 < 64, both[0:32], both[32:64])
        squares = []
        for v in (a, b):
            u = v[0:64].astype(F32) + v[64:128].astype(F32)
            u = u * u
            squares.append(u[:, 0:128] + u[:, 128:256] + (u[:, 256:384] + u[:, 384:512]))
        squares = jnp.concatenate(split(jnp.concatenate(squares, axis=0)), axis=1)
        part[now, j, 32:40] = lax.dot_general(ones, squares, NT, preferred_element_type=F32)

    def send_parts(now):
        for d in range(1, 8):
            j = (me1 + d) % 8
            pltpu.make_async_remote_copy(
                src_ref=part.at[now, j], dst_ref=gather1.at[now, me1],
                send_sem=send1.at[now], recv_sem=recv1.at[now],
                device_id=sharer(j), device_id_type=MESH,
            ).start()
        gather1[now, me1] = part[now, me1]

    def rotations(now):
        bulk(gather1.at[now, pl.ds(0, 7)], recv1.at[now]).wait()
        gather2[now, me2] = tree([gather1[now, s] for s in range(8)])
        for d in range(1, 8):
            pltpu.make_async_remote_copy(
                src_ref=gather2.at[now, me2], dst_ref=gather2.at[now, me2],
                send_sem=send2.at[now], recv_sem=recv2.at[now],
                device_id=holder((me2 + d) % 8), device_id_type=MESH,
            ).start()
        bulk(gather2.at[now, pl.ds(0, 7)], recv2.at[now]).wait()
        total[now, me1] = tree([gather2[now, s] for s in range(8)])
        for d in range(1, 8):
            pltpu.make_async_remote_copy(
                src_ref=total.at[now, me1], dst_ref=total.at[now, me1],
                send_sem=send3.at[now], recv_sem=recv3.at[now],
                device_id=sharer((me1 + d) % 8), device_id_type=MESH,
            ).start()
        bulk(total.at[now, pl.ds(0, 7)], recv3.at[now]).wait()
        bulk(part.at[now, pl.ds(0, 7)], send1.at[now]).wait()
        bulk(gather2.at[now, pl.ds(0, 7)], send2.at[now]).wait()
        bulk(total.at[now, pl.ds(0, 7)], send3.at[now]).wait()

        skews = []
        for j in range(SLOTS):
            packed = total[now, j, 0:32]
            inverse = lax.rsqrt(total[now, j, 32:40] + 1e-06)[0:1]
            turned = pltpu.roll(packed, 64, 1)
            cross = jnp.concatenate(
                [jnp.where(lane32 < 64, packed, turned), jnp.where(lane32 < 64, turned, packed)], axis=0
            )
            column = jnp.sum(jnp.where(lane64 == sub64, inverse, 0.0), axis=1, keepdims=True)
            cosine = jnp.where(lane64 >= 64, cross * inverse, 0.0) * column
            frobenius = jnp.sqrt(jnp.sum(cosine * cosine, axis=(0, 1), keepdims=True))
            upper = jnp.concatenate([cosine * (minus_sign / (1.0 + frobenius)), jnp.zeros((64, 128), F32)], axis=0)
            skews.append(upper - upper.T)
        e0, w0, e1, w1, e2 = [], [], [], [], []
        for k in skews:
            high, low = split(k)
            m = lax.dot_general(
                jnp.concatenate([high, low], axis=1),
                jnp.concatenate(
                    [jnp.concatenate([high, high], axis=1), jnp.concatenate([low, low], axis=1)], axis=0
                ),
                NT, preferred_element_type=F32,
            )
            e0.append(0.5 * (unit - (m[:, 0:128] + m[:, 128:256])))
        for j in range(SLOTS):
            parts = split(e0[j])
            e1.append((product(parts, parts), 0.75 * unit + 0.25 * e0[j]))
            w0.append(product(split(unit + skews[j]), split(unit + 0.5 * e0[j])))
        e1 = [product(split(a), split(b)) for a, b in e1]
        for j in range(SLOTS):
            parts = split(e1[j])
            e2.append((product(parts, parts), 0.75 * unit + 0.25 * e1[j]))
            w1.append(product(split(w0[j]), split(unit + 0.5 * e1[j])))
        e2 = [product(split(a), split(b)) for a, b in e2]
        for j in range(SLOTS):
            r = product(split(w1[j]), split(unit + 0.5 * e2[j])) * (1.0 / math.sqrt(2.0))
            high, low = split(r)
            turn[j, :, 0:128] = high
            turn[j, :, 128:256] = low
            turn[j, :, 256:384] = high

    def apply(now, j):
        a, b = firsts[now], seconds[now]
        high = jnp.concatenate([a[j, 0:WIDTH], b[j, 0:WIDTH]], axis=0)
        low = jnp.concatenate([a[j, WIDTH:], b[j, WIDTH:]], axis=0)
        r = jnp.dot(turn[j], jnp.concatenate([high, high, low], axis=0), preferred_element_type=F32)
        return r[0:WIDTH], r[WIDTH:]

    def put(state, j, v):
        high, low = split(v)
        state[j, 0:WIDTH] = high
        state[j, WIDTH:] = low

    def advance(now):
        later = 1 - now
        first, second = firsts[later], seconds[later]
        a, b = apply(now, SLOTS - 1)
        export[now] = a
        swap = pltpu.make_async_remote_copy(
            src_ref=export.at[now], dst_ref=arrive.at[now],
            send_sem=sendx.at[now], recv_sem=recvx.at[now],
            device_id=(row, sibling), device_id_type=MESH,
        )
        swap.start()
        put(second, SLOTS - 2, b)
        a, b = apply(now, 0)
        put(first, core, a)
        put(first, 1 - core, b)
        for j in range(1, SLOTS - 1):
            a, b = apply(now, j)
            put(first, j + 1, a)
            put(second, j - 1, b)
        for j in range(SLOTS - 1):
            crossing(later, j)
        swap.wait()
        put(second, SLOTS - 1, arrive[now])
        crossing(later, SLOTS - 1)
        send_parts(later)

    def finish():
        for j in range(SLOTS):
            a, b = apply(1, j)
            final[2 * core if j == 0 else min(2 * j + 2, 15)] = a
            final[2 - 2 * core if j == 0 else 2 * j - 1] = b

        def place(d):
            m = ((chip % 4) * 4 + d) % 16
            n = m + m // 15
            n = n + core * (31 - 2 * n)
            return m, n // 2, n % 2

        def start(d, carry):
            m, owner, half = place(d)
            target = out_ref.at[chip, pl.ds(pl.multiple_of(half * WIDTH, WIDTH), WIDTH)]
            arrived = recvf.at[chip, half]

            @pl.when(owner != pair)
            def _():
                pltpu.make_async_remote_copy(
                    src_ref=final.at[m], dst_ref=target, send_sem=sendf.at[m], recv_sem=arrived,
                    device_id=(row, owner), device_id_type=MESH,
                ).start()

            @pl.when(owner == pair)
            def _():
                pltpu.make_async_copy(final.at[m], target, arrived).start()

            return carry

        lax.fori_loop(0, 16, start, 0)

        def sent(d, carry):
            m, owner, half = place(d)

            @pl.when(owner != pair)
            def _():
                bulk(final.at[m], sendf.at[m]).wait()

            return carry

        lax.fori_loop(0, 16, sent, 0)
        for c in range(CHIPS):
            for half in range(2):
                bulk(out_ref.at[c, pl.ds(half * WIDTH, WIDTH)], recvf.at[c, half]).wait()

    for j in range(SLOTS):
        crossing(0, j)
    send_parts(0)

    def two_steps(i, carry):
        rotations(0)
        advance(0)
        rotations(1)

        @pl.when(i < STEPS // 2 - 1)
        def _():
            advance(1)

        @pl.when(i == STEPS // 2 - 1)
        def _():
            finish()

        return carry

    lax.fori_loop(0, STEPS // 2, two_steps, 0)


def per_device(snapshots, start_order):
    rows = snapshots.shape[0]
    wide = 2 * rows
    transposed = snapshots.T.reshape(4 * SLOTS, WIDTH, rows)
    dma = pltpu.SemaphoreType.DMA
    blocks = pl.pallas_call(
        kernel,
        out_shape=jax.ShapeDtypeStruct((CHIPS, 2 * WIDTH, wide), F32),
        in_specs=[pl.BlockSpec(memory_space=pltpu.SMEM), pl.BlockSpec(memory_space=pltpu.VMEM)],
        out_specs=pl.BlockSpec(memory_space=pl.ANY),
        scratch_shapes=[
            pltpu.VMEM((SLOTS, 2 * WIDTH, wide), BF),
            pltpu.VMEM((SLOTS, 2 * WIDTH, wide), BF),
            pltpu.VMEM((SLOTS, 2 * WIDTH, wide), BF),
            pltpu.VMEM((SLOTS, 2 * WIDTH, wide), BF),
            pltpu.VMEM((2, WIDTH, wide), F32),
            pltpu.VMEM((2, WIDTH, wide), F32),
            pltpu.VMEM((2 * SLOTS, WIDTH, rows), F32),
            pltpu.VMEM((2 * SLOTS, WIDTH, rows), F32),
            pltpu.VMEM((2, SLOTS, PART, 128), F32),
            pltpu.VMEM((2, 8, PART, 128), F32),
            pltpu.VMEM((2, 8, PART, 128), F32),
            pltpu.VMEM((2, SLOTS, PART, 128), F32),
            pltpu.VMEM((SLOTS, 128, 384), BF),
            pltpu.VMEM((2 * SLOTS, WIDTH, wide), F32),
            dma((2,)), dma((2,)), dma((2,)), dma((2,)), dma((2,)), dma((2,)), dma((2,)), dma((2,)),
            dma(()), dma(()), dma((2 * SLOTS,)), dma((CHIPS, 2)),
        ],
        compiler_params=pltpu.CompilerParams(
            collective_id=0, has_side_effects=True, vmem_limit_bytes=40 * 1024 * 1024
        ),
    )(start_order, transposed)
    return blocks.transpose(0, 2, 1).reshape(CHIPS * wide, 2 * WIDTH)


def solution(mesh):
    placed = (P(("row", "pair"), None), P())
    return jax.shard_map(
        per_device, mesh=mesh, in_specs=placed, out_specs=P("row", "pair"), check_vma=False
    )
```

```python
import math

import jax
import jax.numpy as jnp
import numpy as np
from jax import lax
from jax.experimental import pallas as pl
from jax.experimental.pallas import tpu as pltpu
from jax.sharding import PartitionSpec as P

STEPS = 12
CHIPS = 8
SLOTS = 8
WIDTH = 64
PART = 40
MESH = pl.DeviceIdType.MESH
BF = jnp.bfloat16
F32 = jnp.float32
NT = (((1,), (1,)), ((), ()))


def split(x):
    high = x.astype(BF)
    return high, (x - high.astype(F32)).astype(BF)


def newton_schulz():
    e0 = np.polynomial.Polynomial([0.5, -0.5])
    e1 = e0 * e0 * (0.75 + 0.25 * e0)
    e2 = e1 * e1 * (0.75 + 0.25 * e1)
    f = (1 + 0.5 * e0) * (1 + 0.5 * e1) * (1 + 0.5 * e2) / math.sqrt(2.0)
    g = np.polynomial.Polynomial(f.coef[1:])(np.polynomial.Polynomial([0.5, 1.0]))
    return float(f.coef[0]), [float(c) for c in g.coef]


ORIGIN, SERIES = newton_schulz()


def dot3(left, right, dims=(((1,), (0,)), ((), ()))):
    axis = dims[0][1][0]
    return lax.dot_general(
        jnp.concatenate([left[0], left[1], left[0]], axis=1),
        jnp.concatenate([right[0], right[0], right[1]], axis=axis),
        dims, preferred_element_type=F32,
    )


def coupling(sums, sign):
    lane = lax.broadcasted_iota(jnp.int32, (32, 128), 1)
    row = lax.broadcasted_iota(jnp.int32, (32, 128), 0)
    left = lane < 64
    inverse = lax.rsqrt(sums[32:40] + 1e-06)
    across = jnp.where(left[0:1], pltpu.roll(inverse, 64, 1)[0:1], inverse[0:1])
    down = jnp.where(
        left,
        jnp.sum(jnp.where(lane == row, inverse[0:1], 0.0), axis=1, keepdims=True),
        jnp.sum(jnp.where(lane == row + 32, inverse[0:1], 0.0), axis=1, keepdims=True),
    )
    cosine = sums[0:32] * across * down
    frobenius = jnp.sqrt(jnp.sum(cosine * cosine, axis=(0, 1), keepdims=True))
    return cosine * (sign / (1.0 + frobenius))


def turn_matrices(packed):
    lane32 = lax.broadcasted_iota(jnp.int32, (32, 128), 1) < 64
    lane = lax.broadcasted_iota(jnp.int32, (64, 128), 1)
    row = lax.broadcasted_iota(jnp.int32, (64, 128), 0)
    left = lane < 64
    right_unit = lane - 64 == row
    unit = ((lane == row) | right_unit).astype(F32)
    keep_left, keep_right = left.astype(F32).astype(BF), (1.0 - left.astype(F32)).astype(BF)
    count = len(packed) // 2

    def swap(v):
        return pltpu.roll(v, 64, 1)

    def diagonal(v):
        return jnp.concatenate([v * keep_left, v * keep_right], axis=0)

    def pairs(v):
        return tuple(diagonal(part) for part in split(v))

    def times(a, b):
        wide = jnp.concatenate(b, axis=1)
        y = jnp.dot(
            jnp.concatenate(split(a), axis=1), jnp.concatenate([wide, wide], axis=0), preferred_element_type=F32
        )
        return y[:, 0:128] + y[:, 128:256]

    def once(a, b):
        return jnp.dot(a.astype(BF), b, preferred_element_type=F32)

    def beside(p, q):
        none = jnp.zeros((64, 128), BF)
        parts = []
        for u, v in zip(split(p), split(q)):
            parts.append(
                jnp.concatenate([jnp.concatenate([u, none], axis=1), jnp.concatenate([none, v], axis=1)], axis=0)
            )
        return parts

    couplings, bases = [], []
    for p, q in zip(packed[::2], packed[1::2]):
        couplings.append(
            jnp.concatenate([jnp.where(lane32, p, swap(q)), jnp.where(lane32, swap(p), q)], axis=0)
        )
    for c in couplings:
        parts = split(c)
        bases.append(dot3(parts, tuple(diagonal(part) for part in parts), NT))
    t1 = [b - 0.5 * unit for b in bases]
    d1 = [pairs(t) for t in t1]
    t2 = [times(t, d) for t, d in zip(t1, d1)]
    t3 = [times(t, d) for t, d in zip(t2, d1)]
    t4 = [once(t, diagonal(t.astype(BF))) for t in t2]
    d4 = [diagonal(t.astype(BF)) for t in t4]

    def cubic(i, k):
        return SERIES[k] * unit + SERIES[k + 1] * t1[i] + (SERIES[k + 2] * t2[i] + SERIES[k + 3] * t3[i])

    g = [cubic(i, 8) + SERIES[12] * t4[i] for i in range(count)]
    g = [cubic(i, 4) + once(v, d) for i, (v, d) in enumerate(zip(g, d4))]
    g = [cubic(i, 0) + once(v, d) for i, (v, d) in enumerate(zip(g, d4))]
    turned = [swap(c) for c in couplings]
    upright = [jnp.concatenate([c, s], axis=0).T[0:64] for c, s in zip(couplings, turned)]
    out = []
    for i in range(count):
        b, c, s = bases[i], couplings[i], turned[i]
        y = dot3(split(g[i]), beside(jnp.where(left, b, s), jnp.where(left, swap(b), c)))
        tops = [y[:, 0:128] + jnp.where(lane == row, ORIGIN, 0.0), y[:, 128:256] + jnp.where(lane == row, ORIGIN, 0.0)]
        y = dot3(split(jnp.concatenate([upright[i], b], axis=0)), beside(*tops))
        for h in range(2):
            z = y[:, 128 * h : 128 * h + 128]
            top = jnp.where(left, tops[h], -(ORIGIN * (s, c)[h] + z[64:128]))
            bottom = z[0:64] + jnp.where(right_unit, ORIGIN, 0.0)
            out.append(jnp.concatenate([top, bottom], axis=0))
    return out


def tree(pieces):
    while len(pieces) > 1:
        pieces = [a + b for a, b in zip(pieces[::2], pieces[1::2])]
    return pieces[0]


def kernel(
    order_ref, xt_ref, out_ref,
    first0, first1, second0, second1, export, arrive, outbox, inbox, part, gather1, gather2, total, leave, turn, final,
    send1, recv1, send2, recv2, send3, recv3, sendx, recvx, sendb, recvb, sendf, recvf,
):
    row = lax.axis_index("row")
    pair = lax.axis_index("pair")
    z, y_low = row // 2, row % 2
    chip, core = pair // 2, pair % 2
    x, y_high = chip // 2, chip % 2
    side = (y_low + y_high) % 2
    sibling = pair + 1 - 2 * core
    firsts, seconds = (first0, first1), (second0, second1)
    along_x, along_z = [], []
    for d, e in ((2, 1), (1, 1), (3, 1), (2, 0), (0, 1), (1, 0), (3, 0)):
        u, v = (x + d) % 4, (side + e) % 2
        along_x.append((u * 2 + v, z * 2 + (v + y_high) % 2, u * 2 + y_high))
        u, v = (z + d) % 4, (y_high + e) % 2
        along_z.append((u * 2 + v, u * 2 + (side + v) % 2, x * 2 + v))
    sharers, holders = (along_x, along_z), (along_z, along_x)
    mine, held = (x * 2 + side, z * 2 + y_high), (z * 2 + y_high, x * 2 + side)

    lanes = xt_ref.shape[2]
    here = pl.ds(pl.multiple_of(core * lanes, lanes), lanes)
    there = pl.ds(pl.multiple_of((1 - core) * lanes, lanes), lanes)

    barrier = pltpu.get_barrier_semaphore()

    def greet(device):
        pl.semaphore_signal(barrier, inc=1, device_id=device, device_id_type=MESH)

    for _, r, c in along_x + along_z:
        greet((r, 2 * c))
        greet((r, 2 * c + 1))
    for d in range(1, 2 * CHIPS):
        greet((row, (pair + d) % (2 * CHIPS)))

    def position(owner, block):
        plain = 2 * (block % SLOTS) + block // SLOTS
        return plain + owner * (31 - 2 * plain)

    for b in range(2 * SLOTS):
        outbox[b] = xt_ref[order_ref[position(1 - core, b)]]
    pl.semaphore_wait(barrier, 28 + 2 * CHIPS - 1)
    swap = pltpu.make_async_remote_copy(
        src_ref=outbox, dst_ref=inbox, send_sem=sendb, recv_sem=recvb,
        device_id=(row, sibling), device_id_type=MESH,
    )
    swap.start()
    for b in range(2 * SLOTS):
        high, low = split(xt_ref[order_ref[position(core, b)]])
        state = first0 if b < SLOTS else second0
        state[b % SLOTS, 0:WIDTH, here] = high
        state[b % SLOTS, WIDTH:, here] = low
    swap.wait()
    for b in range(2 * SLOTS):
        high, low = split(inbox[b])
        state = first0 if b < SLOTS else second0
        state[b % SLOTS, 0:WIDTH, there] = high
        state[b % SLOTS, WIDTH:, there] = low

    lane32 = lax.broadcasted_iota(jnp.int32, (32, 128), 1)
    ones = jnp.ones((8, 256), BF)

    def bulk(buffer, sem):
        return pltpu.make_async_copy(buffer, buffer, sem)

    def crossing(now, j):
        a = firsts[now][j]
        b = seconds[now][j]
        grown = lax.dot_general(a, b, NT, preferred_element_type=F32)
        grown = grown[0:64] + grown[64:128]
        both = grown + pltpu.roll(grown, 64, 1)
        part[now, j, 0:32] = jnp.where(lane32 < 64, both[0:32], both[32:64])
        squares = []
        for v in (a, b):
            u = v[0:64].astype(F32) + v[64:128].astype(F32)
            u = u * u
            squares.append(u[:, 0:128] + u[:, 128:256] + (u[:, 256:384] + u[:, 384:512]))
        squares = jnp.concatenate(split(jnp.concatenate(squares, axis=0)), axis=1)
        part[now, j, 32:40] = lax.dot_general(ones, squares, NT, preferred_element_type=F32)

    def send(source, target, sends, arrivals, device):
        pltpu.make_async_remote_copy(
            src_ref=source, dst_ref=target, send_sem=sends, recv_sem=arrivals,
            device_id=device, device_id_type=MESH,
        ).start()

    def send_parts(now):
        for k in range(2):

            @pl.when(core == k)
            def _():
                for j, r, c in sharers[k]:
                    send(part.at[now, j], gather1.at[now, k, mine[k]], send1.at[now], recv1.at[now, k], (r, 2 * c + 1))
                if k:
                    gather1[now, k, mine[k]] = part[now, mine[k]]
                else:
                    send(
                        part.at[now, mine[k]], gather1.at[now, k, mine[k]], send1.at[now], recv1.at[now, k],
                        (row, sibling),
                    )

    def rotations(now):
        @pl.when(core == 1)
        def _():
            for k in (1, 0):
                bulk(gather1.at[now, k, pl.ds(0, 8 - k)], recv1.at[now, k]).wait()
                gather2[now, k, held[k]] = tree([gather1[now, k, s] for s in range(8)])
                for _, r, c in holders[k]:
                    place = gather2.at[now, k, held[k]]
                    send(place, place, send2.at[now], recv2.at[now, k], (r, 2 * c + 1))
            for k in (1, 0):
                bulk(gather2.at[now, k, pl.ds(0, 7)], recv2.at[now, k]).wait()
                found = coupling(tree([gather2[now, k, s] for s in range(8)]), 1.0 - 2.0 * k)
                place = total.at[now, mine[k]]
                if k:
                    total[now, mine[k]] = found
                    source = place
                else:
                    leave[now] = found
                    source = leave.at[now]
                for _, r, c in sharers[k]:
                    send(source, place, send3.at[now], recv3.at[now], (r, 2 * c + k))
                if not k:
                    send(source, place, send3.at[now], recv3.at[now], (row, sibling))
            bulk(total.at[now, pl.ds(0, 7)], recv3.at[now]).wait()
            bulk(part.at[now, pl.ds(0, 7)], send1.at[now]).wait()
            for k in range(2):
                bulk(gather2.at[now, k, pl.ds(0, 7)], send2.at[now]).wait()
            bulk(total.at[now], send3.at[now]).wait()
            bulk(total.at[now, pl.ds(0, 7)], send3.at[now]).wait()

        @pl.when(core == 0)
        def _():
            bulk(total.at[now], recv3.at[now]).wait()
            bulk(part.at[now], send1.at[now]).wait()

        turns = turn_matrices([total[now, j] for j in range(SLOTS)])
        for j in range(SLOTS):
            high, low = split(turns[j])
            turn[j, :, 0:128] = high
            turn[j, :, 128:256] = low
            turn[j, :, 256:384] = high

    def apply(now, j):
        a, b = firsts[now], seconds[now]
        high = jnp.concatenate([a[j, 0:WIDTH], b[j, 0:WIDTH]], axis=0)
        low = jnp.concatenate([a[j, WIDTH:], b[j, WIDTH:]], axis=0)
        r = jnp.dot(turn[j], jnp.concatenate([high, high, low], axis=0), preferred_element_type=F32)
        return r[0:WIDTH], r[WIDTH:]

    def put(state, j, v):
        high, low = split(v)
        state[j, 0:WIDTH] = high
        state[j, WIDTH:] = low

    def advance(now):
        later = 1 - now
        first, second = firsts[later], seconds[later]
        a, b = apply(now, SLOTS - 1)
        export[now] = a
        swap = pltpu.make_async_remote_copy(
            src_ref=export.at[now], dst_ref=arrive.at[now],
            send_sem=sendx.at[now], recv_sem=recvx.at[now],
            device_id=(row, sibling), device_id_type=MESH,
        )
        swap.start()
        put(second, SLOTS - 2, b)
        a, b = apply(now, 0)
        put(first, core, a)
        put(first, 1 - core, b)
        for j in range(1, SLOTS - 1):
            a, b = apply(now, j)
            put(first, j + 1, a)
            put(second, j - 1, b)
        for j in range(SLOTS - 1):
            crossing(later, j)
        swap.wait()
        put(second, SLOTS - 1, arrive[now])
        crossing(later, SLOTS - 1)
        send_parts(later)

    def finish():
        for j in range(SLOTS):
            a, b = apply(1, j)
            final[2 * core if j == 0 else min(2 * j + 2, 15)] = a
            final[2 - 2 * core if j == 0 else 2 * j - 1] = b

        def place(d):
            m = ((chip % 4) * 4 + d) % 16
            n = m + m // 15
            n = n + core * (31 - 2 * n)
            return m, n // 2, n % 2

        def start(d, carry):
            m, owner, half = place(d)
            target = out_ref.at[chip, pl.ds(pl.multiple_of(half * WIDTH, WIDTH), WIDTH)]
            arrived = recvf.at[chip, half]

            @pl.when(owner != pair)
            def _():
                pltpu.make_async_remote_copy(
                    src_ref=final.at[m], dst_ref=target, send_sem=sendf.at[m], recv_sem=arrived,
                    device_id=(row, owner), device_id_type=MESH,
                ).start()

            @pl.when(owner == pair)
            def _():
                pltpu.make_async_copy(final.at[m], target, arrived).start()

            return carry

        lax.fori_loop(0, 16, start, 0)

        def sent(d, carry):
            m, owner, half = place(d)

            @pl.when(owner != pair)
            def _():
                bulk(final.at[m], sendf.at[m]).wait()

            return carry

        lax.fori_loop(0, 16, sent, 0)
        for c in range(CHIPS):
            for half in range(2):
                bulk(out_ref.at[c, pl.ds(half * WIDTH, WIDTH)], recvf.at[c, half]).wait()

    for j in range(SLOTS):
        crossing(0, j)
    send_parts(0)

    def two_steps(i, carry):
        rotations(0)
        advance(0)
        rotations(1)

        @pl.when(i < STEPS // 2 - 1)
        def _():
            advance(1)

        @pl.when(i == STEPS // 2 - 1)
        def _():
            finish()

        return carry

    lax.fori_loop(0, STEPS // 2, two_steps, 0)


def per_device(snapshots, start_order):
    rows = snapshots.shape[0]
    wide = 2 * rows
    transposed = snapshots.T.reshape(4 * SLOTS, WIDTH, rows)
    dma = pltpu.SemaphoreType.DMA
    blocks = pl.pallas_call(
        kernel,
        out_shape=jax.ShapeDtypeStruct((CHIPS, 2 * WIDTH, wide), F32),
        in_specs=[pl.BlockSpec(memory_space=pltpu.SMEM), pl.BlockSpec(memory_space=pltpu.VMEM)],
        out_specs=pl.BlockSpec(memory_space=pl.ANY),
        scratch_shapes=[
            pltpu.VMEM((SLOTS, 2 * WIDTH, wide), BF),
            pltpu.VMEM((SLOTS, 2 * WIDTH, wide), BF),
            pltpu.VMEM((SLOTS, 2 * WIDTH, wide), BF),
            pltpu.VMEM((SLOTS, 2 * WIDTH, wide), BF),
            pltpu.VMEM((2, WIDTH, wide), F32),
            pltpu.VMEM((2, WIDTH, wide), F32),
            pltpu.VMEM((2 * SLOTS, WIDTH, rows), F32),
            pltpu.VMEM((2 * SLOTS, WIDTH, rows), F32),
            pltpu.VMEM((2, SLOTS, PART, 128), F32),
            pltpu.VMEM((2, 2, 8, PART, 128), F32),
            pltpu.VMEM((2, 2, 8, PART, 128), F32),
            pltpu.VMEM((2, SLOTS, 32, 128), F32),
            pltpu.VMEM((2, 32, 128), F32),
            pltpu.VMEM((SLOTS, 128, 384), BF),
            pltpu.VMEM((2 * SLOTS, WIDTH, wide), F32),
            dma((2,)), dma((2, 2)), dma((2,)), dma((2, 2)), dma((2,)), dma((2,)), dma((2,)), dma((2,)),
            dma(()), dma(()), dma((2 * SLOTS,)), dma((CHIPS, 2)),
        ],
        compiler_params=pltpu.CompilerParams(
            collective_id=0, has_side_effects=True, vmem_limit_bytes=40 * 1024 * 1024
        ),
    )(start_order, transposed)
    return blocks.transpose(0, 2, 1).reshape(CHIPS * wide, 2 * WIDTH)


def solution(mesh):
    placed = (P(("row", "pair"), None), P())
    return jax.shard_map(
        per_device, mesh=mesh, in_specs=placed, out_specs=P("row", "pair"), check_vma=False
    )
```

```python
import math

import jax
import jax.numpy as jnp
import numpy as np
from jax import lax
from jax.experimental import pallas as pl
from jax.experimental.pallas import tpu as pltpu
from jax.sharding import PartitionSpec as P

STEPS = 12
CHIPS = 8
SLOTS = 8
WIDTH = 64
PART = 33
MESH = pl.DeviceIdType.MESH
BF = jnp.bfloat16
F32 = jnp.float32
NT = (((1,), (1,)), ((), ()))


def split(x):
    high = x.astype(BF)
    return high, (x - high.astype(F32)).astype(BF)


def newton_schulz():
    e0 = np.polynomial.Polynomial([0.5, -0.5])
    e1 = e0 * e0 * (0.75 + 0.25 * e0)
    e2 = e1 * e1 * (0.75 + 0.25 * e1)
    f = (1 + 0.5 * e0) * (1 + 0.5 * e1) * (1 + 0.5 * e2) / math.sqrt(2.0)
    g = np.polynomial.Polynomial(f.coef[1:])(np.polynomial.Polynomial([0.5, 1.0]))
    return float(f.coef[0]), [float(c) for c in g.coef]


ORIGIN, SERIES = newton_schulz()


def dot3(left, right, dims=(((1,), (0,)), ((), ()))):
    axis = dims[0][1][0]
    return lax.dot_general(
        jnp.concatenate([left[0], left[1], left[0]], axis=1),
        jnp.concatenate([right[0], right[0], right[1]], axis=axis),
        dims, preferred_element_type=F32,
    )


def coupling(sums, sign):
    lane = lax.broadcasted_iota(jnp.int32, (32, 128), 1)
    row = lax.broadcasted_iota(jnp.int32, (32, 128), 0)
    left = lane < 64
    inverse = lax.rsqrt(jnp.broadcast_to(sums[32:33], (8, 128)) + 1e-06)
    across = jnp.where(left[0:1], pltpu.roll(inverse, 64, 1)[0:1], inverse[0:1])
    down = jnp.where(
        left,
        jnp.sum(jnp.where(lane == row, inverse[0:1], 0.0), axis=1, keepdims=True),
        jnp.sum(jnp.where(lane == row + 32, inverse[0:1], 0.0), axis=1, keepdims=True),
    )
    cosine = sums[0:32] * across * down
    frobenius = jnp.sqrt(jnp.sum(cosine * cosine, axis=(0, 1), keepdims=True))
    return cosine * (sign / (1.0 + frobenius))


def turn_matrices(packed):
    lane32 = lax.broadcasted_iota(jnp.int32, (32, 128), 1) < 64
    lane = lax.broadcasted_iota(jnp.int32, (64, 128), 1)
    row = lax.broadcasted_iota(jnp.int32, (64, 128), 0)
    left = lane < 64
    right_unit = lane - 64 == row
    unit = ((lane == row) | right_unit).astype(F32)
    keep_left, keep_right = left.astype(F32).astype(BF), (1.0 - left.astype(F32)).astype(BF)
    count = len(packed) // 2

    def swap(v):
        return pltpu.roll(v, 64, 1)

    def diagonal(v):
        return jnp.concatenate([v * keep_left, v * keep_right], axis=0)

    def pairs(v):
        return tuple(diagonal(part) for part in split(v))

    def times(a, b):
        wide = jnp.concatenate(b, axis=1)
        y = jnp.dot(
            jnp.concatenate(split(a), axis=1), jnp.concatenate([wide, wide], axis=0), preferred_element_type=F32
        )
        return y[:, 0:128] + y[:, 128:256]

    def once(a, b):
        return jnp.dot(a.astype(BF), b, preferred_element_type=F32)

    def beside(p, q):
        none = jnp.zeros((64, 128), BF)
        parts = []
        for u, v in zip(split(p), split(q)):
            parts.append(
                jnp.concatenate([jnp.concatenate([u, none], axis=1), jnp.concatenate([none, v], axis=1)], axis=0)
            )
        return parts

    couplings, bases = [], []
    for p, q in zip(packed[::2], packed[1::2]):
        couplings.append(
            jnp.concatenate([jnp.where(lane32, p, swap(q)), jnp.where(lane32, swap(p), q)], axis=0)
        )
    for c in couplings:
        parts = split(c)
        bases.append(dot3(parts, tuple(diagonal(part) for part in parts), NT))
    t1 = [b - 0.5 * unit for b in bases]
    d1 = [pairs(t) for t in t1]
    t2 = [times(t, d) for t, d in zip(t1, d1)]
    t3 = [times(t, d) for t, d in zip(t2, d1)]
    t4 = [once(t, diagonal(t.astype(BF))) for t in t2]
    d4 = [diagonal(t.astype(BF)) for t in t4]

    def cubic(i, k):
        return SERIES[k] * unit + SERIES[k + 1] * t1[i] + (SERIES[k + 2] * t2[i] + SERIES[k + 3] * t3[i])

    g = [cubic(i, 8) + SERIES[12] * t4[i] for i in range(count)]
    g = [cubic(i, 4) + once(v, d) for i, (v, d) in enumerate(zip(g, d4))]
    g = [cubic(i, 0) + once(v, d) for i, (v, d) in enumerate(zip(g, d4))]
    turned = [swap(c) for c in couplings]
    upright = [jnp.concatenate([c, s], axis=0).T[0:64] for c, s in zip(couplings, turned)]
    out = []
    for i in range(count):
        b, c, s = bases[i], couplings[i], turned[i]
        y = dot3(split(g[i]), beside(jnp.where(left, b, s), jnp.where(left, swap(b), c)))
        tops = [y[:, 0:128] + jnp.where(lane == row, ORIGIN, 0.0), y[:, 128:256] + jnp.where(lane == row, ORIGIN, 0.0)]
        y = dot3(split(jnp.concatenate([upright[i], b], axis=0)), beside(*tops))
        for h in range(2):
            z = y[:, 128 * h : 128 * h + 128]
            top = jnp.where(left, tops[h], -(ORIGIN * (s, c)[h] + z[64:128]))
            bottom = z[0:64] + jnp.where(right_unit, ORIGIN, 0.0)
            out.append(jnp.concatenate([top, bottom], axis=0))
    return out


def tree(pieces):
    while len(pieces) > 1:
        pieces = [a + b for a, b in zip(pieces[::2], pieces[1::2])]
    return pieces[0]


def kernel(
    order_ref, x_ref, out_ref,
    loaded, xt_ref, first0, first1, second0, second1, export, arrive, outbox, inbox, part, gather1, gather2, total, leave, turn, final,
    send1, recv1, send2, recv2, send3, recv3, sendx, recvx, sendb, recvb, sendf, recvf, loads,
):
    row = lax.axis_index("row")
    pair = lax.axis_index("pair")
    z, y_low = row // 2, row % 2
    chip, core = pair // 2, pair % 2
    x, y_high = chip // 2, chip % 2
    side = (y_low + y_high) % 2
    sibling = pair + 1 - 2 * core
    firsts, seconds = (first0, first1), (second0, second1)
    along_x, along_z = [], []
    for d, e in ((2, 1), (1, 1), (3, 1), (2, 0), (0, 1), (1, 0), (3, 0)):
        u, v = (x + d) % 4, (side + e) % 2
        along_x.append((u * 2 + v, z * 2 + (v + y_high) % 2, u * 2 + y_high))
        u, v = (z + d) % 4, (y_high + e) % 2
        along_z.append((u * 2 + v, u * 2 + (side + v) % 2, x * 2 + v))
    sharers, holders = (along_x, along_z), (along_z, along_x)
    mine, held = (x * 2 + side, z * 2 + y_high), (z * 2 + y_high, x * 2 + side)

    lanes = xt_ref.shape[2]
    here = pl.ds(pl.multiple_of(core * lanes, lanes), lanes)
    there = pl.ds(pl.multiple_of((1 - core) * lanes, lanes), lanes)

    chunk = loaded.shape[1] // 4
    columns = [pl.ds(chunk * q, chunk) for q in range(4)]
    copies = [pltpu.make_async_copy(x_ref.at[:, c], loaded.at[:, c], loads.at[q]) for q, c in enumerate(columns)]
    for copy in copies:
        copy.start()
    barrier = pltpu.get_barrier_semaphore()

    def greet(device):
        pl.semaphore_signal(barrier, inc=1, device_id=device, device_id_type=MESH)

    for _, r, c in along_x + along_z:
        greet((r, 2 * c))
        greet((r, 2 * c + 1))
    for d in range(1, 2 * CHIPS):
        greet((row, (pair + d) % (2 * CHIPS)))

    for q, copy in enumerate(copies):
        copy.wait()
        for u in range(chunk // 128 * q, chunk // 128 * (q + 1)):
            tile = loaded[:, 128 * u : 128 * u + 128].T
            xt_ref[2 * u] = tile[0:WIDTH]
            xt_ref[2 * u + 1] = tile[WIDTH:]

    def position(owner, block):
        plain = 2 * (block % SLOTS) + block // SLOTS
        return plain + owner * (31 - 2 * plain)

    for b in range(2 * SLOTS):
        outbox[b] = xt_ref[order_ref[position(1 - core, b)]]
    pl.semaphore_wait(barrier, 28 + 2 * CHIPS - 1)
    swap = pltpu.make_async_remote_copy(
        src_ref=outbox, dst_ref=inbox, send_sem=sendb, recv_sem=recvb,
        device_id=(row, sibling), device_id_type=MESH,
    )
    swap.start()
    for b in range(2 * SLOTS):
        high, low = split(xt_ref[order_ref[position(core, b)]])
        state = first0 if b < SLOTS else second0
        state[b % SLOTS, 0:WIDTH, here] = high
        state[b % SLOTS, WIDTH:, here] = low
    swap.wait()
    for b in range(2 * SLOTS):
        high, low = split(inbox[b])
        state = first0 if b < SLOTS else second0
        state[b % SLOTS, 0:WIDTH, there] = high
        state[b % SLOTS, WIDTH:, there] = low

    lane32 = lax.broadcasted_iota(jnp.int32, (32, 128), 1)
    ones = jnp.ones((8, 256), BF)

    def bulk(buffer, sem):
        return pltpu.make_async_copy(buffer, buffer, sem)

    def crossing(now, j):
        a = firsts[now][j]
        b = seconds[now][j]
        grown = lax.dot_general(a, b, NT, preferred_element_type=F32)
        grown = grown[0:64] + grown[64:128]
        both = grown + pltpu.roll(grown, 64, 1)
        part[now, j, 0:32] = jnp.where(lane32 < 64, both[0:32], both[32:64])
        squares = []
        for v in (a, b):
            u = v[0:64].astype(F32) + v[64:128].astype(F32)
            u = u * u
            squares.append(u[:, 0:128] + u[:, 128:256] + (u[:, 256:384] + u[:, 384:512]))
        squares = jnp.concatenate(split(jnp.concatenate(squares, axis=0)), axis=1)
        part[now, j, 32:33] = lax.dot_general(ones, squares, NT, preferred_element_type=F32)[0:1]

    def send(source, target, sends, arrivals, device):
        pltpu.make_async_remote_copy(
            src_ref=source, dst_ref=target, send_sem=sends, recv_sem=arrivals,
            device_id=device, device_id_type=MESH,
        ).start()

    def send_parts(now):
        for k in range(2):

            @pl.when(core == k)
            def _():
                for j, r, c in sharers[k]:
                    send(part.at[now, j], gather1.at[now, k, mine[k]], send1.at[now], recv1.at[now, k], (r, 2 * c + 1))
                if k:
                    gather1[now, k, mine[k]] = part[now, mine[k]]
                else:
                    send(
                        part.at[now, mine[k]], gather1.at[now, k, mine[k]], send1.at[now], recv1.at[now, k],
                        (row, sibling),
                    )

    def rotations(now):
        @pl.when(core == 1)
        def _():
            for k in (1, 0):
                bulk(gather1.at[now, k, pl.ds(0, 8 - k)], recv1.at[now, k]).wait()
                gather2[now, k, held[k]] = tree([gather1[now, k, s] for s in range(8)])
                for _, r, c in holders[k]:
                    place = gather2.at[now, k, held[k]]
                    send(place, place, send2.at[now], recv2.at[now, k], (r, 2 * c + 1))
            for k in (1, 0):
                bulk(gather2.at[now, k, pl.ds(0, 7)], recv2.at[now, k]).wait()
                found = coupling(tree([gather2[now, k, s] for s in range(8)]), 1.0 - 2.0 * k)
                place = total.at[now, mine[k]]
                if k:
                    total[now, mine[k]] = found
                    source = place
                else:
                    leave[now] = found
                    source = leave.at[now]
                for _, r, c in sharers[k]:
                    send(source, place, send3.at[now], recv3.at[now], (r, 2 * c + k))
                if not k:
                    send(source, place, send3.at[now], recv3.at[now], (row, sibling))
            bulk(total.at[now, pl.ds(0, 7)], recv3.at[now]).wait()
            bulk(part.at[now, pl.ds(0, 7)], send1.at[now]).wait()
            for k in range(2):
                bulk(gather2.at[now, k, pl.ds(0, 7)], send2.at[now]).wait()
            bulk(total.at[now], send3.at[now]).wait()
            bulk(total.at[now, pl.ds(0, 7)], send3.at[now]).wait()

        @pl.when(core == 0)
        def _():
            bulk(total.at[now], recv3.at[now]).wait()
            bulk(part.at[now], send1.at[now]).wait()

        turns = turn_matrices([total[now, j] for j in range(SLOTS)])
        for j in range(SLOTS):
            high, low = split(turns[j])
            turn[j, :, 0:128] = high
            turn[j, :, 128:256] = low
            turn[j, :, 256:384] = high

    def apply(now, j):
        a, b = firsts[now], seconds[now]
        high = jnp.concatenate([a[j, 0:WIDTH], b[j, 0:WIDTH]], axis=0)
        low = jnp.concatenate([a[j, WIDTH:], b[j, WIDTH:]], axis=0)
        r = jnp.dot(turn[j], jnp.concatenate([high, high, low], axis=0), preferred_element_type=F32)
        return r[0:WIDTH], r[WIDTH:]

    def put(state, j, v):
        high, low = split(v)
        state[j, 0:WIDTH] = high
        state[j, WIDTH:] = low

    def advance(now):
        later = 1 - now
        first, second = firsts[later], seconds[later]
        a, b = apply(now, SLOTS - 1)
        export[now] = a
        swap = pltpu.make_async_remote_copy(
            src_ref=export.at[now], dst_ref=arrive.at[now],
            send_sem=sendx.at[now], recv_sem=recvx.at[now],
            device_id=(row, sibling), device_id_type=MESH,
        )
        swap.start()
        put(second, SLOTS - 2, b)
        a, b = apply(now, 0)
        put(first, core, a)
        put(first, 1 - core, b)
        for j in range(1, SLOTS - 1):
            a, b = apply(now, j)
            put(first, j + 1, a)
            put(second, j - 1, b)
        for j in range(SLOTS - 1):
            crossing(later, j)
        swap.wait()
        put(second, SLOTS - 1, arrive[now])
        crossing(later, SLOTS - 1)
        send_parts(later)

    def finish():
        for j in range(SLOTS):
            a, b = apply(1, j)
            final[2 * core if j == 0 else min(2 * j + 2, 15)] = a
            final[2 - 2 * core if j == 0 else 2 * j - 1] = b

        def place(d):
            m = ((chip + d) % 4) * 4 + d // 4
            n = m + m // 15
            n = n + core * (31 - 2 * n)
            return m, n // 2, n % 2

        def start(d, carry):
            m, owner, half = place(d)
            target = out_ref.at[chip, pl.ds(pl.multiple_of(half * WIDTH, WIDTH), WIDTH)]
            arrived = recvf.at[chip, half]

            @pl.when(owner != pair)
            def _():
                pltpu.make_async_remote_copy(
                    src_ref=final.at[m], dst_ref=target, send_sem=sendf.at[m], recv_sem=arrived,
                    device_id=(row, owner), device_id_type=MESH,
                ).start()

            @pl.when(owner == pair)
            def _():
                pltpu.make_async_copy(final.at[m], target, arrived).start()

            return carry

        lax.fori_loop(0, 16, start, 0)

        def sent(d, carry):
            m, owner, half = place(d)

            @pl.when(owner != pair)
            def _():
                bulk(final.at[m], sendf.at[m]).wait()

            return carry

        lax.fori_loop(0, 16, sent, 0)
        for c in range(CHIPS):
            for half in range(2):
                bulk(out_ref.at[c, pl.ds(half * WIDTH, WIDTH)], recvf.at[c, half]).wait()

    for j in range(SLOTS):
        crossing(0, j)
    send_parts(0)

    def two_steps(i, carry):
        rotations(0)
        advance(0)
        rotations(1)

        @pl.when(i < STEPS // 2 - 1)
        def _():
            advance(1)

        @pl.when(i == STEPS // 2 - 1)
        def _():
            finish()

        return carry

    lax.fori_loop(0, STEPS // 2, two_steps, 0)


def per_device(snapshots, start_order):
    rows = snapshots.shape[0]
    wide = 2 * rows
    dma = pltpu.SemaphoreType.DMA
    blocks = pl.pallas_call(
        kernel,
        out_shape=jax.ShapeDtypeStruct((CHIPS, 2 * WIDTH, wide), F32),
        in_specs=[pl.BlockSpec(memory_space=pltpu.SMEM), pl.BlockSpec(memory_space=pl.ANY)],
        out_specs=pl.BlockSpec(memory_space=pl.ANY),
        scratch_shapes=[
            pltpu.VMEM(snapshots.shape, F32),
            pltpu.VMEM((4 * SLOTS, WIDTH, rows), F32),
            pltpu.VMEM((SLOTS, 2 * WIDTH, wide), BF),
            pltpu.VMEM((SLOTS, 2 * WIDTH, wide), BF),
            pltpu.VMEM((SLOTS, 2 * WIDTH, wide), BF),
            pltpu.VMEM((SLOTS, 2 * WIDTH, wide), BF),
            pltpu.VMEM((2, WIDTH, wide), F32),
            pltpu.VMEM((2, WIDTH, wide), F32),
            pltpu.VMEM((2 * SLOTS, WIDTH, rows), F32),
            pltpu.VMEM((2 * SLOTS, WIDTH, rows), F32),
            pltpu.VMEM((2, SLOTS, PART, 128), F32),
            pltpu.VMEM((2, 2, 8, PART, 128), F32),
            pltpu.VMEM((2, 2, 8, PART, 128), F32),
            pltpu.VMEM((2, SLOTS, 32, 128), F32),
            pltpu.VMEM((2, 32, 128), F32),
            pltpu.VMEM((SLOTS, 128, 384), BF),
            pltpu.VMEM((2 * SLOTS, WIDTH, wide), F32),
            dma((2,)), dma((2, 2)), dma((2,)), dma((2, 2)), dma((2,)), dma((2,)), dma((2,)), dma((2,)),
            dma(()), dma(()), dma((2 * SLOTS,)), dma((CHIPS, 2)), dma((4,)),
        ],
        compiler_params=pltpu.CompilerParams(
            collective_id=0, has_side_effects=True, vmem_limit_bytes=40 * 1024 * 1024
        ),
    )(start_order, snapshots)
    return blocks.transpose(0, 2, 1).reshape(CHIPS * wide, 2 * WIDTH)


def solution(mesh):
    placed = (P(("row", "pair"), None), P())
    return jax.shard_map(
        per_device, mesh=mesh, in_specs=placed, out_specs=P("row", "pair"), check_vma=False
    )
```

```python
import math

import jax
import jax.numpy as jnp
import numpy as np
from jax import lax
from jax.experimental import pallas as pl
from jax.experimental.pallas import tpu as pltpu
from jax.sharding import PartitionSpec as P

STEPS = 12
CHIPS = 8
SLOTS = 8
WIDTH = 64
PART = 33
MESH = pl.DeviceIdType.MESH
BF = jnp.bfloat16
F32 = jnp.float32
NT = (((1,), (1,)), ((), ()))


def split(x):
    high = x.astype(BF)
    return high, (x - high.astype(F32)).astype(BF)


def newton_schulz():
    e0 = np.polynomial.Polynomial([0.5, -0.5])
    e1 = e0 * e0 * (0.75 + 0.25 * e0)
    e2 = e1 * e1 * (0.75 + 0.25 * e1)
    f = (1 + 0.5 * e0) * (1 + 0.5 * e1) * (1 + 0.5 * e2) / math.sqrt(2.0)
    g = np.polynomial.Polynomial(f.coef[1:])(np.polynomial.Polynomial([0.5, 1.0]))
    return float(f.coef[0]), [float(c) for c in g.coef]


ORIGIN, SERIES = newton_schulz()


def dot3(left, right, dims=(((1,), (0,)), ((), ()))):
    axis = dims[0][1][0]
    return lax.dot_general(
        jnp.concatenate([left[0], left[1], left[0]], axis=1),
        jnp.concatenate([right[0], right[0], right[1]], axis=axis),
        dims, preferred_element_type=F32,
    )


def coupling(sums, sign):
    lane = lax.broadcasted_iota(jnp.int32, (32, 128), 1)
    row = lax.broadcasted_iota(jnp.int32, (32, 128), 0)
    left = lane < 64
    inverse = lax.rsqrt(jnp.broadcast_to(sums[32:33], (8, 128)) + 1e-06)
    across = jnp.where(left[0:1], pltpu.roll(inverse, 64, 1)[0:1], inverse[0:1])
    down = jnp.where(
        left,
        jnp.sum(jnp.where(lane == row, inverse[0:1], 0.0), axis=1, keepdims=True),
        jnp.sum(jnp.where(lane == row + 32, inverse[0:1], 0.0), axis=1, keepdims=True),
    )
    cosine = sums[0:32] * across * down
    frobenius = jnp.sqrt(jnp.sum(cosine * cosine, axis=(0, 1), keepdims=True))
    return cosine * (sign / (1.0 + frobenius))


def turn_matrices(packed):
    lane32 = lax.broadcasted_iota(jnp.int32, (32, 128), 1) < 64
    lane = lax.broadcasted_iota(jnp.int32, (64, 128), 1)
    row = lax.broadcasted_iota(jnp.int32, (64, 128), 0)
    left = lane < 64
    right_unit = lane - 64 == row
    unit = ((lane == row) | right_unit).astype(F32)
    keep_left, keep_right = left.astype(F32).astype(BF), (1.0 - left.astype(F32)).astype(BF)
    count = len(packed) // 2

    def swap(v):
        return pltpu.roll(v, 64, 1)

    def diagonal(v):
        return jnp.concatenate([v * keep_left, v * keep_right], axis=0)

    def pairs(v):
        return tuple(diagonal(part) for part in split(v))

    def times(a, b):
        wide = jnp.concatenate(b, axis=1)
        y = jnp.dot(
            jnp.concatenate(split(a), axis=1), jnp.concatenate([wide, wide], axis=0), preferred_element_type=F32
        )
        return y[:, 0:128] + y[:, 128:256]

    def once(a, b):
        return jnp.dot(a.astype(BF), b, preferred_element_type=F32)

    def beside(p, q):
        none = jnp.zeros((64, 128), BF)
        parts = []
        for u, v in zip(split(p), split(q)):
            parts.append(
                jnp.concatenate([jnp.concatenate([u, none], axis=1), jnp.concatenate([none, v], axis=1)], axis=0)
            )
        return parts

    couplings, bases = [], []
    for p, q in zip(packed[::2], packed[1::2]):
        couplings.append(
            jnp.concatenate([jnp.where(lane32, p, swap(q)), jnp.where(lane32, swap(p), q)], axis=0)
        )
    for c in couplings:
        parts = split(c)
        bases.append(dot3(parts, tuple(diagonal(part) for part in parts), NT))
    t1 = [b - 0.5 * unit for b in bases]
    d1 = [pairs(t) for t in t1]
    t2 = [times(t, d) for t, d in zip(t1, d1)]
    t3 = [times(t, d) for t, d in zip(t2, d1)]
    t4 = [once(t, diagonal(t.astype(BF))) for t in t2]
    d4 = [diagonal(t.astype(BF)) for t in t4]

    def cubic(i, k):
        return SERIES[k] * unit + SERIES[k + 1] * t1[i] + (SERIES[k + 2] * t2[i] + SERIES[k + 3] * t3[i])

    g = [cubic(i, 8) + SERIES[12] * t4[i] for i in range(count)]
    g = [cubic(i, 4) + once(v, d) for i, (v, d) in enumerate(zip(g, d4))]
    g = [cubic(i, 0) + once(v, d) for i, (v, d) in enumerate(zip(g, d4))]
    turned = [swap(c) for c in couplings]
    upright = [jnp.concatenate([c, s], axis=0).T[0:64] for c, s in zip(couplings, turned)]

    def pair_of(i):
        b, c, s = bases[i], couplings[i], turned[i]
        y = dot3(split(g[i]), beside(jnp.where(left, b, s), jnp.where(left, swap(b), c)))
        tops = [y[:, 0:128] + jnp.where(lane == row, ORIGIN, 0.0), y[:, 128:256] + jnp.where(lane == row, ORIGIN, 0.0)]
        y = dot3(split(jnp.concatenate([upright[i], b], axis=0)), beside(*tops))
        out = []
        for h in range(2):
            z = y[:, 128 * h : 128 * h + 128]
            top = jnp.where(left, tops[h], -(ORIGIN * (s, c)[h] + z[64:128]))
            bottom = z[0:64] + jnp.where(right_unit, ORIGIN, 0.0)
            out.append(jnp.concatenate([top, bottom], axis=0))
        return out

    return pair_of


def tree(pieces):
    while len(pieces) > 1:
        pieces = [a + b for a, b in zip(pieces[::2], pieces[1::2])]
    return pieces[0]


def kernel(
    order_ref, x_ref, out_ref,
    loaded, xt_ref, first0, first1, second0, second1, export, arrive, outbox, inbox, part, gather1, gather2, total, leave, turn, final,
    send1, recv1, send2, recv2, send3, recv3, sendx, recvx, sendb, recvb, sendf, recvf, loads,
):
    row = lax.axis_index("row")
    pair = lax.axis_index("pair")
    z, y_low = row // 2, row % 2
    chip, core = pair // 2, pair % 2
    x, y_high = chip // 2, chip % 2
    side = (y_low + y_high) % 2
    sibling = pair + 1 - 2 * core
    firsts, seconds = (first0, first1), (second0, second1)
    along_x, along_z = [], []
    for d, e in ((2, 1), (1, 1), (3, 1), (2, 0), (0, 1), (1, 0), (3, 0)):
        u, v = (x + d) % 4, (side + e) % 2
        along_x.append((u * 2 + v, z * 2 + (v + y_high) % 2, u * 2 + y_high))
        u, v = (z + d) % 4, (y_high + e) % 2
        along_z.append((u * 2 + v, u * 2 + (side + v) % 2, x * 2 + v))
    sharers, holders = (along_x, along_z), (along_z, along_x)
    mine, held = (x * 2 + side, z * 2 + y_high), (z * 2 + y_high, x * 2 + side)

    lanes = xt_ref.shape[2]
    here = pl.ds(pl.multiple_of(core * lanes, lanes), lanes)
    there = pl.ds(pl.multiple_of((1 - core) * lanes, lanes), lanes)

    chunk = loaded.shape[1] // 4
    columns = [pl.ds(chunk * q, chunk) for q in range(4)]
    copies = [pltpu.make_async_copy(x_ref.at[:, c], loaded.at[:, c], loads.at[q]) for q, c in enumerate(columns)]
    for copy in copies:
        copy.start()
    barrier = pltpu.get_barrier_semaphore()

    def greet(device):
        pl.semaphore_signal(barrier, inc=1, device_id=device, device_id_type=MESH)

    for _, r, c in along_x + along_z:
        greet((r, 2 * c))
        greet((r, 2 * c + 1))
    for d in range(1, 2 * CHIPS):
        greet((row, (pair + d) % (2 * CHIPS)))

    for q, copy in enumerate(copies):
        copy.wait()
        for u in range(chunk // 128 * q, chunk // 128 * (q + 1)):
            tile = loaded[:, 128 * u : 128 * u + 128].T
            xt_ref[2 * u] = tile[0:WIDTH]
            xt_ref[2 * u + 1] = tile[WIDTH:]

    def position(owner, block):
        plain = 2 * (block % SLOTS) + block // SLOTS
        return plain + owner * (31 - 2 * plain)

    for b in range(2 * SLOTS):
        outbox[b] = xt_ref[order_ref[position(1 - core, b)]]
    pl.semaphore_wait(barrier, 28 + 2 * CHIPS - 1)
    swap = pltpu.make_async_remote_copy(
        src_ref=outbox, dst_ref=inbox, send_sem=sendb, recv_sem=recvb,
        device_id=(row, sibling), device_id_type=MESH,
    )
    swap.start()
    for b in range(2 * SLOTS):
        high, low = split(xt_ref[order_ref[position(core, b)]])
        state = first0 if b < SLOTS else second0
        state[b % SLOTS, 0:WIDTH, here] = high
        state[b % SLOTS, WIDTH:, here] = low
    swap.wait()
    for b in range(2 * SLOTS):
        high, low = split(inbox[b])
        state = first0 if b < SLOTS else second0
        state[b % SLOTS, 0:WIDTH, there] = high
        state[b % SLOTS, WIDTH:, there] = low

    lane32 = lax.broadcasted_iota(jnp.int32, (32, 128), 1)
    lane8 = lax.broadcasted_iota(jnp.int32, (8, 128), 1) < 64

    def bulk(buffer, sem):
        return pltpu.make_async_copy(buffer, buffer, sem)

    def sums_of_squares(u):
        u = u * u
        u = u[:, 0:128] + u[:, 128:256] + (u[:, 256:384] + u[:, 384:512])
        return jnp.broadcast_to(jnp.sum(u.T, axis=0, keepdims=True), (8, 128))

    def crossing(now, j, norms=None):
        a = firsts[now][j]
        b = seconds[now][j]
        grown = lax.dot_general(a, b, NT, preferred_element_type=F32)
        grown = grown[0:64] + grown[64:128]
        both = grown + pltpu.roll(grown, 64, 1)
        part[now, j, 0:32] = jnp.where(lane32 < 64, both[0:32], both[32:64])
        if norms is None:
            norms = sums_of_squares(
                jnp.concatenate([v[0:64].astype(F32) + v[64:128].astype(F32) for v in (a, b)], axis=0)
            )
        part[now, j, 32:33] = norms[0:1]

    def send(source, target, sends, arrivals, device):
        pltpu.make_async_remote_copy(
            src_ref=source, dst_ref=target, send_sem=sends, recv_sem=arrivals,
            device_id=device, device_id_type=MESH,
        ).start()

    def send_parts(now):
        for k in range(2):

            @pl.when(core == k)
            def _():
                for j, r, c in sharers[k]:
                    send(part.at[now, j], gather1.at[now, k, mine[k]], send1.at[now], recv1.at[now, k], (r, 2 * c + 1))
                if k:
                    gather1[now, k, mine[k]] = part[now, mine[k]]
                else:
                    send(
                        part.at[now, mine[k]], gather1.at[now, k, mine[k]], send1.at[now], recv1.at[now, k],
                        (row, sibling),
                    )

    def rotations(now):
        @pl.when(core == 1)
        def _():
            for k in (1, 0):
                bulk(gather1.at[now, k, pl.ds(0, 8 - k)], recv1.at[now, k]).wait()
                gather2[now, k, held[k]] = tree([gather1[now, k, s] for s in range(8)])
                for _, r, c in holders[k]:
                    place = gather2.at[now, k, held[k]]
                    send(place, place, send2.at[now], recv2.at[now, k], (r, 2 * c + 1))
            for k in (1, 0):
                bulk(gather2.at[now, k, pl.ds(0, 7)], recv2.at[now, k]).wait()
                found = coupling(tree([gather2[now, k, s] for s in range(8)]), 1.0 - 2.0 * k)
                place = total.at[now, mine[k]]
                if k:
                    total[now, mine[k]] = found
                    source = place
                else:
                    leave[now] = found
                    source = leave.at[now]
                for _, r, c in sharers[k]:
                    send(source, place, send3.at[now], recv3.at[now], (r, 2 * c + k))
                if not k:
                    send(source, place, send3.at[now], recv3.at[now], (row, sibling))
            bulk(total.at[now, pl.ds(0, 7)], recv3.at[now]).wait()
            bulk(part.at[now, pl.ds(0, 7)], send1.at[now]).wait()
            for k in range(2):
                bulk(gather2.at[now, k, pl.ds(0, 7)], send2.at[now]).wait()
            bulk(total.at[now], send3.at[now]).wait()
            bulk(total.at[now, pl.ds(0, 7)], send3.at[now]).wait()

        @pl.when(core == 0)
        def _():
            bulk(total.at[now], recv3.at[now]).wait()
            bulk(part.at[now], send1.at[now]).wait()

        return turn_matrices([total[now, j] for j in range(SLOTS)])

    def keep(pair_of, i):
        for j, r in zip((2 * i, 2 * i + 1), pair_of(i)):
            high, low = split(r)
            turn[j, :, 0:128] = high
            turn[j, :, 128:256] = low
            turn[j, :, 256:384] = high

    def apply(now, j):
        a, b = firsts[now], seconds[now]
        high = jnp.concatenate([a[j, 0:WIDTH], b[j, 0:WIDTH]], axis=0)
        low = jnp.concatenate([a[j, WIDTH:], b[j, WIDTH:]], axis=0)
        r = jnp.dot(turn[j], jnp.concatenate([high, high, low], axis=0), preferred_element_type=F32)
        return r[0:WIDTH], r[WIDTH:], sums_of_squares(r)

    def put(state, j, v):
        high, low = split(v)
        state[j, 0:WIDTH] = high
        state[j, WIDTH:] = low

    def advance(now, pair_of):
        later = 1 - now
        first, second = firsts[later], seconds[later]
        keep(pair_of, SLOTS // 2 - 1)
        norms = [None] * SLOTS
        a, b, norms[7] = apply(now, SLOTS - 1)
        export[now] = a
        swap = pltpu.make_async_remote_copy(
            src_ref=export.at[now], dst_ref=arrive.at[now],
            send_sem=sendx.at[now], recv_sem=recvx.at[now],
            device_id=(row, sibling), device_id_type=MESH,
        )
        swap.start()
        put(second, SLOTS - 2, b)
        for i in range(SLOTS // 2 - 1):
            keep(pair_of, i)
        a, b, norms[0] = apply(now, 0)
        put(first, core, a)
        put(first, 1 - core, b)
        for j in range(1, SLOTS - 1):
            a, b, norms[j] = apply(now, j)
            put(first, j + 1, a)
            put(second, j - 1, b)
        halves = norms[0], pltpu.roll(norms[0], 64, 1)
        lead = [jnp.where(core == 0, *halves), jnp.where(core == 0, halves[1], halves[0])] + norms[1 : SLOTS - 1]
        for j in range(SLOTS - 1):
            crossing(later, j, jnp.where(lane8, lead[j], norms[j + 1]))
        swap.wait()
        came = arrive[now]
        put(second, SLOTS - 1, came)
        crossing(later, SLOTS - 1, jnp.where(lane8, lead[SLOTS - 1], sums_of_squares(jnp.concatenate([came, came], axis=0))))
        send_parts(later)

    def finish(pair_of):
        for i in range(SLOTS // 2):
            keep(pair_of, i)
        for j in range(SLOTS):
            a, b, _ = apply(1, j)
            final[2 * core if j == 0 else min(2 * j + 2, 15)] = a
            final[2 - 2 * core if j == 0 else 2 * j - 1] = b

        def place(d):
            m = ((chip + d) % 4) * 4 + d // 4
            n = m + m // 15
            n = n + core * (31 - 2 * n)
            return m, n // 2, n % 2

        def start(d, carry):
            m, owner, half = place(d)
            target = out_ref.at[chip, pl.ds(pl.multiple_of(half * WIDTH, WIDTH), WIDTH)]
            arrived = recvf.at[chip, half]

            @pl.when(owner != pair)
            def _():
                pltpu.make_async_remote_copy(
                    src_ref=final.at[m], dst_ref=target, send_sem=sendf.at[m], recv_sem=arrived,
                    device_id=(row, owner), device_id_type=MESH,
                ).start()

            @pl.when(owner == pair)
            def _():
                pltpu.make_async_copy(final.at[m], target, arrived).start()

            return carry

        lax.fori_loop(0, 16, start, 0)

        def sent(d, carry):
            m, owner, half = place(d)

            @pl.when(owner != pair)
            def _():
                bulk(final.at[m], sendf.at[m]).wait()

            return carry

        lax.fori_loop(0, 16, sent, 0)
        for c in range(CHIPS):
            for half in range(2):
                bulk(out_ref.at[c, pl.ds(half * WIDTH, WIDTH)], recvf.at[c, half]).wait()

    for j in range(SLOTS):
        crossing(0, j)
    send_parts(0)

    def two_steps(i, carry):
        advance(0, rotations(0))
        pair_of = rotations(1)

        @pl.when(i < STEPS // 2 - 1)
        def _():
            advance(1, pair_of)

        @pl.when(i == STEPS // 2 - 1)
        def _():
            finish(pair_of)

        return carry

    lax.fori_loop(0, STEPS // 2, two_steps, 0)


def per_device(snapshots, start_order):
    rows = snapshots.shape[0]
    wide = 2 * rows
    dma = pltpu.SemaphoreType.DMA
    blocks = pl.pallas_call(
        kernel,
        out_shape=jax.ShapeDtypeStruct((CHIPS, 2 * WIDTH, wide), F32),
        in_specs=[pl.BlockSpec(memory_space=pltpu.SMEM), pl.BlockSpec(memory_space=pl.ANY)],
        out_specs=pl.BlockSpec(memory_space=pl.ANY),
        scratch_shapes=[
            pltpu.VMEM(snapshots.shape, F32),
            pltpu.VMEM((4 * SLOTS, WIDTH, rows), F32),
            pltpu.VMEM((SLOTS, 2 * WIDTH, wide), BF),
            pltpu.VMEM((SLOTS, 2 * WIDTH, wide), BF),
            pltpu.VMEM((SLOTS, 2 * WIDTH, wide), BF),
            pltpu.VMEM((SLOTS, 2 * WIDTH, wide), BF),
            pltpu.VMEM((2, WIDTH, wide), F32),
            pltpu.VMEM((2, WIDTH, wide), F32),
            pltpu.VMEM((2 * SLOTS, WIDTH, rows), F32),
            pltpu.VMEM((2 * SLOTS, WIDTH, rows), F32),
            pltpu.VMEM((2, SLOTS, PART, 128), F32),
            pltpu.VMEM((2, 2, 8, PART, 128), F32),
            pltpu.VMEM((2, 2, 8, PART, 128), F32),
            pltpu.VMEM((2, SLOTS, 32, 128), F32),
            pltpu.VMEM((2, 32, 128), F32),
            pltpu.VMEM((SLOTS, 128, 384), BF),
            pltpu.VMEM((2 * SLOTS, WIDTH, wide), F32),
            dma((2,)), dma((2, 2)), dma((2,)), dma((2, 2)), dma((2,)), dma((2,)), dma((2,)), dma((2,)),
            dma(()), dma(()), dma((2 * SLOTS,)), dma((CHIPS, 2)), dma((4,)),
        ],
        compiler_params=pltpu.CompilerParams(
            collective_id=0, has_side_effects=True, vmem_limit_bytes=40 * 1024 * 1024
        ),
    )(start_order, snapshots)
    return blocks.transpose(0, 2, 1).reshape(CHIPS * wide, 2 * WIDTH)


def solution(mesh):
    placed = (P(("row", "pair"), None), P())
    return jax.shard_map(
        per_device, mesh=mesh, in_specs=placed, out_specs=P("row", "pair"), check_vma=False
    )
```

```python
import math

import jax
import jax.numpy as jnp
import numpy as np
from jax import lax
from jax.experimental import pallas as pl
from jax.experimental.pallas import tpu as pltpu
from jax.sharding import PartitionSpec as P

STEPS = 12
CHIPS = 8
SLOTS = 8
WIDTH = 64
PART = 33
MESH = pl.DeviceIdType.MESH
BF = jnp.bfloat16
F32 = jnp.float32
NT = (((1,), (1,)), ((), ()))


def split(x):
    high = x.astype(BF)
    return high, (x - high.astype(F32)).astype(BF)


def newton_schulz():
    e0 = np.polynomial.Polynomial([0.5, -0.5])
    e1 = e0 * e0 * (0.75 + 0.25 * e0)
    e2 = e1 * e1 * (0.75 + 0.25 * e1)
    f = (1 + 0.5 * e0) * (1 + 0.5 * e1) * (1 + 0.5 * e2) / math.sqrt(2.0)
    g = np.polynomial.Polynomial(f.coef[1:])(np.polynomial.Polynomial([0.5, 1.0]))
    return float(f.coef[0]), [float(c) for c in g.coef]


ORIGIN, SERIES = newton_schulz()


def dot3(left, right, dims=(((1,), (0,)), ((), ()))):
    axis = dims[0][1][0]
    return lax.dot_general(
        jnp.concatenate([left[0], left[1], left[0]], axis=1),
        jnp.concatenate([right[0], right[0], right[1]], axis=axis),
        dims, preferred_element_type=F32,
    )


def coupling(sums, sign):
    lane = lax.broadcasted_iota(jnp.int32, (32, 128), 1)
    row = lax.broadcasted_iota(jnp.int32, (32, 128), 0)
    left = lane < 64
    inverse = lax.rsqrt(jnp.broadcast_to(sums[32:33], (8, 128)) + 1e-06)
    across = jnp.where(left[0:1], pltpu.roll(inverse, 64, 1)[0:1], inverse[0:1])
    down = jnp.where(
        left,
        jnp.sum(jnp.where(lane == row, inverse[0:1], 0.0), axis=1, keepdims=True),
        jnp.sum(jnp.where(lane == row + 32, inverse[0:1], 0.0), axis=1, keepdims=True),
    )
    cosine = sums[0:32] * across * down
    squares = jnp.sum(tree([cosine[i : i + 8] * cosine[i : i + 8] for i in range(0, 32, 8)]), axis=0, keepdims=True)
    frobenius = jnp.sqrt(jnp.sum(squares, axis=1, keepdims=True))
    return cosine * (sign / (1.0 + frobenius))


def turn_matrices(packed):
    lane32 = lax.broadcasted_iota(jnp.int32, (32, 128), 1) < 64
    lane = lax.broadcasted_iota(jnp.int32, (64, 128), 1)
    row = lax.broadcasted_iota(jnp.int32, (64, 128), 0)
    left = lane < 64
    right_unit = lane - 64 == row
    unit = ((lane == row) | right_unit).astype(F32)
    keep_left, keep_right = left.astype(F32).astype(BF), (1.0 - left.astype(F32)).astype(BF)
    count = len(packed) // 2

    def swap(v):
        return pltpu.roll(v, 64, 1)

    def diagonal(v):
        return jnp.concatenate([v * keep_left, v * keep_right], axis=0)

    def pairs(v):
        return tuple(diagonal(part) for part in split(v))

    def times(a, b):
        wide = jnp.concatenate(b, axis=1)
        y = jnp.dot(
            jnp.concatenate(split(a), axis=1), jnp.concatenate([wide, wide], axis=0), preferred_element_type=F32
        )
        return y[:, 0:128] + y[:, 128:256]

    def once(a, b):
        return jnp.dot(a.astype(BF), b, preferred_element_type=F32)

    def beside(p, q):
        none = jnp.zeros((64, 128), BF)
        parts = []
        for u, v in zip(split(p), split(q)):
            parts.append(
                jnp.concatenate([jnp.concatenate([u, none], axis=1), jnp.concatenate([none, v], axis=1)], axis=0)
            )
        return parts

    couplings, bases = [], []
    for p, q in zip(packed[::2], packed[1::2]):
        couplings.append(
            jnp.concatenate([jnp.where(lane32, p, swap(q)), jnp.where(lane32, swap(p), q)], axis=0)
        )
    for c in couplings:
        parts = split(c)
        bases.append(dot3(parts, tuple(diagonal(part) for part in parts), NT))
    turned = [swap(c) for c in couplings]
    uprights = [jnp.concatenate([c, s], axis=0).T[0:64] for c, s in zip(couplings, turned)]
    t1 = [b - 0.5 * unit for b in bases]
    y0 = [jnp.concatenate([u, b], axis=0) for u, b in zip(uprights, bases)]
    both = [times(jnp.concatenate([t, y], axis=0), pairs(t)) for t, y in zip(t1, y0)]
    t2, y1 = [v[0:64] for v in both], [v[64:192] for v in both]
    both = [times(jnp.concatenate([t, a, b], axis=0), pairs(t)) for t, a, b in zip(t2, y0, y1)]
    d4 = [diagonal(v[0:64].astype(BF)) for v in both]
    y2, y3 = [v[64:192] for v in both], [v[192:320] for v in both]

    def cubic(i, k):
        return SERIES[k] * y0[i] + SERIES[k + 1] * y1[i] + (SERIES[k + 2] * y2[i] + SERIES[k + 3] * y3[i])

    y4 = [once(y, d) for y, d in zip(y0, d4)]
    g = [cubic(i, 8) + SERIES[12] * y4[i] for i in range(count)]
    g = [cubic(i, 4) + once(v, d) for i, (v, d) in enumerate(zip(g, d4))]
    g = [cubic(i, 0) + once(v, d) for i, (v, d) in enumerate(zip(g, d4))]
    at_left = jnp.where(lane == row, 1.0, 0.0)
    tops = [beside(jnp.where(left, at_left, s), jnp.where(left, at_left, c)) for c, s in zip(couplings, turned)]
    bottoms = [
        beside(jnp.where(left, b, s), jnp.where(left, swap(b), c)) for b, c, s in zip(bases, couplings, turned)
    ]

    def pair_of(i):
        up = dot3(split(ORIGIN * unit + g[i][64:128]), tops[i])
        down = dot3(split(g[i][0:64]), bottoms[i])
        out = []
        for h, tall in enumerate((uprights[i], swap(uprights[i]))):
            place = slice(128 * h, 128 * h + 128)
            top = jnp.where(left, up[:, place], -up[:, place])
            out.append(
                jnp.concatenate(
                    [top, down[:, place] + ORIGIN * jnp.where(left, tall, jnp.where(right_unit, 1.0, 0.0))], axis=0
                )
            )
        return out

    return pair_of


def tree(pieces):
    while len(pieces) > 1:
        pieces = [a + b for a, b in zip(pieces[::2], pieces[1::2])]
    return pieces[0]


def kernel(
    order_ref, x_ref, out_ref,
    loaded, xt_ref, first0, first1, second0, second1, export, arrive, outbox, inbox, part, gather1, gather2, total, leave, turn, final,
    send1, recv1, send2, recv2, send3, recv3, sendx, recvx, sendb, recvb, sendf, recvf, loads,
):
    row = lax.axis_index("row")
    pair = lax.axis_index("pair")
    z, y_low = row // 2, row % 2
    chip, core = pair // 2, pair % 2
    x, y_high = chip // 2, chip % 2
    side = (y_low + y_high) % 2
    sibling = pair + 1 - 2 * core
    firsts, seconds = (first0, first1), (second0, second1)
    along_x, along_z = [], []
    for d, e in ((2, 1), (1, 1), (3, 1), (2, 0), (0, 1), (1, 0), (3, 0)):
        u, v = (x + d) % 4, (side + e) % 2
        along_x.append((u * 2 + v, z * 2 + (v + y_high) % 2, u * 2 + y_high))
        u, v = (z + d) % 4, (y_high + e) % 2
        along_z.append((u * 2 + v, u * 2 + (side + v) % 2, x * 2 + v))
    sharers, holders = (along_x, along_z), (along_z, along_x)
    mine, held = (x * 2 + side, z * 2 + y_high), (z * 2 + y_high, x * 2 + side)

    lanes = xt_ref.shape[2]
    here = pl.ds(pl.multiple_of(core * lanes, lanes), lanes)
    there = pl.ds(pl.multiple_of((1 - core) * lanes, lanes), lanes)

    chunk = loaded.shape[1] // 4
    columns = [pl.ds(chunk * q, chunk) for q in range(4)]
    copies = [pltpu.make_async_copy(x_ref.at[:, c], loaded.at[:, c], loads.at[q]) for q, c in enumerate(columns)]
    for copy in copies:
        copy.start()
    barrier = pltpu.get_barrier_semaphore()

    def greet(device):
        pl.semaphore_signal(barrier, inc=1, device_id=device, device_id_type=MESH)

    for _, r, c in along_x + along_z:
        greet((r, 2 * c))
        greet((r, 2 * c + 1))
    for d in range(1, 2 * CHIPS):
        greet((row, (pair + d) % (2 * CHIPS)))

    for q, copy in enumerate(copies):
        copy.wait()
        for u in range(chunk // 128 * q, chunk // 128 * (q + 1)):
            tile = loaded[:, 128 * u : 128 * u + 128].T
            xt_ref[2 * u] = tile[0:WIDTH]
            xt_ref[2 * u + 1] = tile[WIDTH:]

    def position(owner, block):
        plain = 2 * (block % SLOTS) + block // SLOTS
        return plain + owner * (31 - 2 * plain)

    for b in range(2 * SLOTS):
        outbox[b] = xt_ref[order_ref[position(1 - core, b)]]
    pl.semaphore_wait(barrier, 28 + 2 * CHIPS - 1)
    swap = pltpu.make_async_remote_copy(
        src_ref=outbox, dst_ref=inbox, send_sem=sendb, recv_sem=recvb,
        device_id=(row, sibling), device_id_type=MESH,
    )
    swap.start()
    for b in range(2 * SLOTS):
        high, low = split(xt_ref[order_ref[position(core, b)]])
        state = first0 if b < SLOTS else second0
        state[b % SLOTS, 0:WIDTH, here] = high
        state[b % SLOTS, WIDTH:, here] = low
    swap.wait()
    for b in range(2 * SLOTS):
        high, low = split(inbox[b])
        state = first0 if b < SLOTS else second0
        state[b % SLOTS, 0:WIDTH, there] = high
        state[b % SLOTS, WIDTH:, there] = low

    lane32 = lax.broadcasted_iota(jnp.int32, (32, 128), 1)
    lane8 = lax.broadcasted_iota(jnp.int32, (8, 128), 1) < 64

    def bulk(buffer, sem):
        return pltpu.make_async_copy(buffer, buffer, sem)

    def sums_of_squares(u):
        u = u * u
        u = u[:, 0:128] + u[:, 128:256] + (u[:, 256:384] + u[:, 384:512])
        return jnp.broadcast_to(jnp.sum(u.T, axis=0, keepdims=True), (8, 128))

    def crossing(now, j, norms=None):
        a = firsts[now][j]
        b = seconds[now][j]
        grown = lax.dot_general(a, b, NT, preferred_element_type=F32)
        grown = grown[0:64] + grown[64:128]
        both = grown + pltpu.roll(grown, 64, 1)
        part[now, j, 0:32] = jnp.where(lane32 < 64, both[0:32], both[32:64])
        if norms is None:
            norms = sums_of_squares(
                jnp.concatenate([v[0:64].astype(F32) + v[64:128].astype(F32) for v in (a, b)], axis=0)
            )
        part[now, j, 32:33] = norms[0:1]

    def send(source, target, sends, arrivals, device):
        pltpu.make_async_remote_copy(
            src_ref=source, dst_ref=target, send_sem=sends, recv_sem=arrivals,
            device_id=device, device_id_type=MESH,
        ).start()

    def send_parts(now):
        for k in range(2):

            @pl.when(core == k)
            def _():
                for j, r, c in sharers[k]:
                    send(part.at[now, j], gather1.at[now, k, mine[k]], send1.at[now], recv1.at[now, k], (r, 2 * c + 1))
                if k:
                    gather1[now, k, mine[k]] = part[now, mine[k]]
                else:
                    send(
                        part.at[now, mine[k]], gather1.at[now, k, mine[k]], send1.at[now], recv1.at[now, k],
                        (row, sibling),
                    )

    def rotations(now):
        @pl.when(core == 1)
        def _():
            for k in (1, 0):
                bulk(gather1.at[now, k, pl.ds(0, 8 - k)], recv1.at[now, k]).wait()
                gather2[now, k, held[k]] = tree([gather1[now, k, s] for s in range(8)])
                for _, r, c in holders[k]:
                    place = gather2.at[now, k, held[k]]
                    send(place, place, send2.at[now], recv2.at[now, k], (r, 2 * c + 1))
            for k in (1, 0):
                bulk(gather2.at[now, k, pl.ds(0, 7)], recv2.at[now, k]).wait()
                found = coupling(tree([gather2[now, k, s] for s in range(8)]), 1.0 - 2.0 * k)
                place = total.at[now, mine[k]]
                if k:
                    total[now, mine[k]] = found
                    source = place
                else:
                    leave[now] = found
                    source = leave.at[now]
                for _, r, c in sharers[k]:
                    send(source, place, send3.at[now], recv3.at[now], (r, 2 * c + k))
                if not k:
                    send(source, place, send3.at[now], recv3.at[now], (row, sibling))
            bulk(total.at[now, pl.ds(0, 7)], recv3.at[now]).wait()
            bulk(part.at[now, pl.ds(0, 7)], send1.at[now]).wait()
            for k in range(2):
                bulk(gather2.at[now, k, pl.ds(0, 7)], send2.at[now]).wait()
            bulk(total.at[now], send3.at[now]).wait()
            bulk(total.at[now, pl.ds(0, 7)], send3.at[now]).wait()

        @pl.when(core == 0)
        def _():
            bulk(total.at[now], recv3.at[now]).wait()
            bulk(part.at[now], send1.at[now]).wait()

        return turn_matrices([total[now, j] for j in range(SLOTS)])

    def keep(pair_of, i):
        for j, r in zip((2 * i, 2 * i + 1), pair_of(i)):
            high, low = split(r)
            turn[j, :, 0:128] = high
            turn[j, :, 128:256] = low
            turn[j, :, 256:384] = high

    def apply(now, j):
        a, b = firsts[now], seconds[now]
        high = jnp.concatenate([a[j, 0:WIDTH], b[j, 0:WIDTH]], axis=0)
        low = jnp.concatenate([a[j, WIDTH:], b[j, WIDTH:]], axis=0)
        r = jnp.dot(turn[j], jnp.concatenate([high, high, low], axis=0), preferred_element_type=F32)
        return r[0:WIDTH], r[WIDTH:], sums_of_squares(r)

    def put(state, j, v):
        high, low = split(v)
        state[j, 0:WIDTH] = high
        state[j, WIDTH:] = low

    def advance(now, pair_of):
        later = 1 - now
        first, second = firsts[later], seconds[later]
        keep(pair_of, SLOTS // 2 - 1)
        norms = [None] * SLOTS
        a, b, norms[7] = apply(now, SLOTS - 1)
        export[now] = a
        swap = pltpu.make_async_remote_copy(
            src_ref=export.at[now], dst_ref=arrive.at[now],
            send_sem=sendx.at[now], recv_sem=recvx.at[now],
            device_id=(row, sibling), device_id_type=MESH,
        )
        swap.start()
        put(second, SLOTS - 2, b)
        for i in range(SLOTS // 2 - 1):
            keep(pair_of, i)
        a, b, norms[0] = apply(now, 0)
        put(first, core, a)
        put(first, 1 - core, b)
        for j in range(1, SLOTS - 1):
            a, b, norms[j] = apply(now, j)
            put(first, j + 1, a)
            put(second, j - 1, b)
        halves = norms[0], pltpu.roll(norms[0], 64, 1)
        lead = [jnp.where(core == 0, *halves), jnp.where(core == 0, halves[1], halves[0])] + norms[1 : SLOTS - 1]
        for j in range(SLOTS - 1):
            crossing(later, j, jnp.where(lane8, lead[j], norms[j + 1]))
        swap.wait()
        came = arrive[now]
        put(second, SLOTS - 1, came)
        crossing(later, SLOTS - 1, jnp.where(lane8, lead[SLOTS - 1], sums_of_squares(jnp.concatenate([came, came], axis=0))))
        send_parts(later)

    def finish(pair_of):
        for i in range(SLOTS // 2):
            keep(pair_of, i)
        for j in range(SLOTS):
            a, b, _ = apply(1, j)
            final[2 * core if j == 0 else min(2 * j + 2, 15)] = a
            final[2 - 2 * core if j == 0 else 2 * j - 1] = b

        def place(d):
            m = ((chip + d) % 4) * 4 + d // 4
            n = m + m // 15
            n = n + core * (31 - 2 * n)
            return m, n // 2, n % 2

        def start(d, carry):
            m, owner, half = place(d)
            target = out_ref.at[chip, pl.ds(pl.multiple_of(half * WIDTH, WIDTH), WIDTH)]
            arrived = recvf.at[chip, half]

            @pl.when(owner != pair)
            def _():
                pltpu.make_async_remote_copy(
                    src_ref=final.at[m], dst_ref=target, send_sem=sendf.at[m], recv_sem=arrived,
                    device_id=(row, owner), device_id_type=MESH,
                ).start()

            @pl.when(owner == pair)
            def _():
                pltpu.make_async_copy(final.at[m], target, arrived).start()

            return carry

        lax.fori_loop(0, 16, start, 0)

        def sent(d, carry):
            m, owner, half = place(d)

            @pl.when(owner != pair)
            def _():
                bulk(final.at[m], sendf.at[m]).wait()

            return carry

        lax.fori_loop(0, 16, sent, 0)
        for c in range(CHIPS):
            for half in range(2):
                bulk(out_ref.at[c, pl.ds(half * WIDTH, WIDTH)], recvf.at[c, half]).wait()

    for j in range(SLOTS):
        crossing(0, j)
    send_parts(0)

    def two_steps(i, carry):
        advance(0, rotations(0))
        pair_of = rotations(1)

        @pl.when(i < STEPS // 2 - 1)
        def _():
            advance(1, pair_of)

        @pl.when(i == STEPS // 2 - 1)
        def _():
            finish(pair_of)

        return carry

    lax.fori_loop(0, STEPS // 2, two_steps, 0)


def per_device(snapshots, start_order):
    rows = snapshots.shape[0]
    wide = 2 * rows
    dma = pltpu.SemaphoreType.DMA
    blocks = pl.pallas_call(
        kernel,
        out_shape=jax.ShapeDtypeStruct((CHIPS, 2 * WIDTH, wide), F32),
        in_specs=[pl.BlockSpec(memory_space=pltpu.SMEM), pl.BlockSpec(memory_space=pl.ANY)],
        out_specs=pl.BlockSpec(memory_space=pl.ANY),
        scratch_shapes=[
            pltpu.VMEM(snapshots.shape, F32),
            pltpu.VMEM((4 * SLOTS, WIDTH, rows), F32),
            pltpu.VMEM((SLOTS, 2 * WIDTH, wide), BF),
            pltpu.VMEM((SLOTS, 2 * WIDTH, wide), BF),
            pltpu.VMEM((SLOTS, 2 * WIDTH, wide), BF),
            pltpu.VMEM((SLOTS, 2 * WIDTH, wide), BF),
            pltpu.VMEM((2, WIDTH, wide), F32),
            pltpu.VMEM((2, WIDTH, wide), F32),
            pltpu.VMEM((2 * SLOTS, WIDTH, rows), F32),
            pltpu.VMEM((2 * SLOTS, WIDTH, rows), F32),
            pltpu.VMEM((2, SLOTS, PART, 128), F32),
            pltpu.VMEM((2, 2, 8, PART, 128), F32),
            pltpu.VMEM((2, 2, 8, PART, 128), F32),
            pltpu.VMEM((2, SLOTS, 32, 128), F32),
            pltpu.VMEM((2, 32, 128), F32),
            pltpu.VMEM((SLOTS, 128, 384), BF),
            pltpu.VMEM((2 * SLOTS, WIDTH, wide), F32),
            dma((2,)), dma((2, 2)), dma((2,)), dma((2, 2)), dma((2,)), dma((2,)), dma((2,)), dma((2,)),
            dma(()), dma(()), dma((2 * SLOTS,)), dma((CHIPS, 2)), dma((4,)),
        ],
        compiler_params=pltpu.CompilerParams(
            collective_id=0, has_side_effects=True, vmem_limit_bytes=40 * 1024 * 1024
        ),
    )(start_order, snapshots)
    return blocks.transpose(0, 2, 1).reshape(CHIPS * wide, 2 * WIDTH)


def solution(mesh):
    placed = (P(("row", "pair"), None), P())
    return jax.shard_map(
        per_device, mesh=mesh, in_specs=placed, out_specs=P("row", "pair"), check_vma=False
    )
```
